32 devices in a mesh: row: 4 (over y, x), col: 8 (over z, core).
Axes of the slice: x: 2, y: 2, z: 4, core: 2. Of those that a mesh axis runs over, the one named last changes fastest.
Arguments:
- matrix: float32 [6, 4, 128, 128, 8, 128], P(None, 'row', None, None, 'col'), may hold values from -6 to 6
- factors: float32 [10, 512, 512], P(None, None, 'col'), as said below
- starts: int32 [10], replicated, may hold values from 0 to 2560, as said below
Outputs:
- updated: float32 [6, 4, 128, 128, 8, 128], P(None, 'row', None, None, 'col')
The draws below stay inside these ranges and needn't reach their ends.
Inputs may be any that keep to these rules, and one draw needn't show every extreme that they name: starts[w] = starts[0] + 256 * w, and starts[0] is a multiple of 128. Each factors[w] is orthogonal.
All inputs are finite; a program needn't handle non-finite values.
Results may differ from the reference program's by a relative error of at most 0.0001.
Values sent between devices are 32-bit elements; how exact they have to be, the bound alone decides.
No kernel may reach another device: no remote copies, remote signals or barrier semaphores. Data moves between devices by JAX's collectives and lax.ppermute only.
A program may use at most 384 MiB of HBM per device.

```python
import jax
import jax.numpy as jnp
from jax import lax

ORDER = 131072
ROWS = 3072
NB = 128
WIN = 512
SHIFT = 256
WINS = 10
RCYC = 6
CCYC = 128
N_ROW = 4
N_COL = 8


def draw_factors(key, part):
    normal_draw = jax.random.normal(key, (WINS, WIN, WIN), jnp.float32)
    ortho_part, upper_part = jnp.linalg.qr(normal_draw)
    return ortho_part.astype(jnp.float32)


def draw_starts(key, part):
    choices_count = (ROWS - (WIN + SHIFT * (WINS - 1))) // NB + 1
    base_tile = jax.random.randint(jax.random.fold_in(key, 7), (), 0, choices_count, dtype=jnp.int32)
    return (base_tile * NB + SHIFT * jnp.arange(WINS, dtype=jnp.int32)).astype(jnp.int32)


def steps_of(rng, extent, pieces, smallest, top_value):
    def one(dim, blocks):
        steps = jax.random.uniform(jax.random.fold_in(jax.random.fold_in(rng, 6), dim), (blocks,), jnp.float32, smallest / len(pieces), top_value / len(pieces))
        return jnp.repeat(jnp.exp(steps), extent[dim] // blocks).reshape((-1,) + (1,) * (len(extent) - dim - 1))

    gain = one(*pieces[0])
    for cut in pieces[1:]:
        gain = gain * one(*cut)
    return gain


def gaussian(key, shape, deviation, bound, split=(), kind=jnp.bfloat16):
    values = deviation * jax.random.normal(key, shape, jnp.float32)
    if split:
        values = values * steps_of(key, shape, split, -0.22, 0.18)
    return jnp.clip(values, -bound, bound).astype(kind)


def setup_inputs(seed: int = 0) -> dict:
    seeds = jax.random.split(jax.random.key(seed), 4)
    matrix = gaussian(seeds[0], (RCYC, N_ROW, NB, CCYC, N_COL, NB), 1.0, 6.0, ((1, 4), (4, 8)), jnp.float32)
    factors = draw_factors(jax.random.fold_in(seeds[3], 71), 0)
    starts = draw_starts(jax.random.fold_in(seeds[3], 71), 0)
    return dict(matrix=matrix, factors=factors, starts=starts)


def reference(matrix, factors, starts):
    matrix_rows = matrix.reshape(ROWS, ORDER)
    for window in range(WINS):
        offset_row = starts[window].astype(jnp.int32)
        window_rows = lax.dynamic_slice_in_dim(matrix_rows, offset_row, WIN, 0)
        result_rows = jnp.dot(factors[window].T.astype(jnp.float32), window_rows.astype(jnp.float32), precision=lax.Precision.HIGHEST, preferred_element_type=jnp.float32)
        matrix_rows = lax.dynamic_update_slice_in_dim(matrix_rows, result_rows, offset_row, 0)
    for window in range(WINS):
        offset_col = starts[window].astype(jnp.int32)
        window_cols = lax.dynamic_slice_in_dim(matrix_rows, offset_col, WIN, 1)
        result_cols = jnp.dot(window_cols.astype(jnp.float32), factors[window].astype(jnp.float32), precision=lax.Precision.HIGHEST, preferred_element_type=jnp.float32)
        matrix_rows = lax.dynamic_update_slice_in_dim(matrix_rows, result_cols, offset_col, 1)
    return matrix_rows.reshape(matrix.shape)
```

```python
import functools

import jax
import jax.numpy as jnp
from jax import lax
from jax.experimental import pallas as pl
from jax.experimental.pallas import tpu as pltpu
from jax.sharding import PartitionSpec as P

SHIFT = 256
CHUNKS = 4
GROUP = 2


def split(values):
    high = values.astype(jnp.bfloat16)
    low = (values - high.astype(jnp.float32)).astype(jnp.bfloat16)
    return high, low


def prepare_kernel(gathered, high_ref, low_ref):
    parts, each = gathered.shape[0], gathered.shape[2]
    for part in range(parts):
        high, low = split(gathered[part, 0])
        high_ref[0, pl.ds(part * each, each), :] = high
        low_ref[0, pl.ds(part * each, each), :] = low


def prepare(gathered):
    parts, wins, each, win = gathered.shape
    shape = jax.ShapeDtypeStruct((wins, win, win), jnp.bfloat16)
    spec = pl.BlockSpec((1, win, win), lambda w: (w, 0, 0))
    return pl.pallas_call(
        prepare_kernel,
        grid=(wins,),
        in_specs=[pl.BlockSpec((parts, 1, each, win), lambda w: (0, w, 0, 0))],
        out_specs=[spec, spec],
        out_shape=[shape, shape],
        name="prepare",
    )(gathered)


def left_kernel(peers, scalars, high_ref, low_ref, *refs):
    pieces, outs = refs[:peers], refs[peers : 2 * peers]
    band, done, in_sem, out_sem = refs[2 * peers :]
    cycles, tile, span, lanes = pieces[0].shape
    group = band.shape[2] // lanes
    steps = span // group
    wins, win, _ = high_ref.shape
    step = pl.program_id(0)
    slot = lax.rem(step, 2)
    me, first = scalars[0], scalars[1]

    def move(at, buffer, sem, into, begin):
        where = lax.rem(at, 2)
        if not begin:
            pltpu.make_async_copy(buffer.at[where], buffer.at[where], sem.at[where]).wait()
            return
        for offset in range(peers):
            source = jnp.bitwise_xor(me, offset)
            for cycle in range(cycles):
                row = pl.multiple_of((cycle * peers + source) * tile, tile)
                for lane in range(group):
                    near = buffer.at[where, pl.ds(row, tile), pl.ds(lane * lanes, lanes)]
                    if into:
                        far = pieces[offset].at[cycle, :, at * group + lane, :]
                        pltpu.make_async_copy(far, near, sem.at[where]).start()
                    else:
                        far = outs[offset].at[cycle, :, at * group + lane, :]
                        pltpu.make_async_copy(near, far, sem.at[where]).start()

    @pl.when(step == 0)
    def _():
        move(step, band, in_sem, True, True)

    @pl.when(step + 1 < steps)
    def _():
        move(step + 1, band, in_sem, True, True)

    @pl.when(step >= 2)
    def _():
        move(step - 2, done, out_sem, False, False)

    move(step, band, in_sem, True, False)
    start = pl.multiple_of(first * tile, tile)
    total = band.shape[1]
    shift = SHIFT
    covered = win + shift * (wins - 1)
    if total > covered:
        done[slot, pl.ds(0, total - covered), :] = band[slot, pl.ds(0, total - covered), :]
        done[slot, pl.ds(covered, total - covered), :] = band[slot, pl.ds(covered, total - covered), :]

    def window(w, _):
        top = pl.multiple_of(start + w * shift, tile)
        rows = pl.ds(top, win)
        x_high, x_low = split(band[slot, rows, :])
        factor = high_ref[w]
        y = jnp.dot(factor, x_high, preferred_element_type=jnp.float32)
        y += jnp.dot(factor, x_low, preferred_element_type=jnp.float32)
        y += jnp.dot(low_ref[w], x_high, preferred_element_type=jnp.float32)
        done[slot, pl.ds(top, shift), :] = y[:shift]
        band[slot, pl.ds(pl.multiple_of(top + shift, tile), win - shift), :] = y[shift:]
        return 0

    lax.fori_loop(0, wins, window, 0)
    last = pl.ds(pl.multiple_of(start + wins * shift, tile), win - shift)
    done[slot, last, :] = band[slot, last, :]
    move(step, done, out_sem, False, True)

    @pl.when(step == steps - 1)
    def _():
        if steps > 1:
            move(step - 1, done, out_sem, False, False)
        move(step, done, out_sem, False, False)


def left(scalars, high, low, pieces):
    peers = len(pieces)
    cycles, tile, span, lanes = pieces[0].shape
    group = GROUP if span % GROUP == 0 else 1
    rows = cycles * peers * tile
    wins, win, _ = high.shape
    whole = pl.BlockSpec(memory_space=pl.ANY)
    resident = pl.BlockSpec((wins, win, win), lambda g, s: (0, 0, 0), pipeline_mode=pl.Buffered(1))
    cols = span * lanes
    return pl.pallas_call(
        functools.partial(left_kernel, peers),
        grid_spec=pltpu.PrefetchScalarGridSpec(
            num_scalar_prefetch=1,
            grid=(span // group,),
            in_specs=[resident, resident] + [whole] * peers,
            out_specs=[whole] * peers,
            scratch_shapes=[
                pltpu.VMEM((2, rows, group * lanes), jnp.float32),
                pltpu.VMEM((2, rows, group * lanes), jnp.float32),
                pltpu.SemaphoreType.DMA((2,)),
                pltpu.SemaphoreType.DMA((2,)),
            ],
        ),
        out_shape=[jax.ShapeDtypeStruct(p.shape, p.dtype) for p in pieces],
        compiler_params=pltpu.CompilerParams(
            dimension_semantics=("arbitrary",), vmem_limit_bytes=48 << 20
        ),
        cost_estimate=pl.CostEstimate(
            flops=6 * wins * win * win * cols,
            bytes_accessed=8 * rows * cols + 4 * wins * win * win,
            transcendentals=0,
        ),
        name="left",
    )(scalars, high, low, *pieces)


def right_kernel(scalars, high_ref, low_ref, picked, out, band):
    parts, cycles, rows, lanes = picked.shape
    wins, win, _ = high_ref.shape
    shift = SHIFT
    for part in range(parts):
        for cycle in range(cycles):
            band[cycle * parts + part] = picked[part, cycle]
    first = scalars[1]
    tiles, pace = win // lanes, shift // lanes

    def window(w, _):
        top = first + w * pace
        x = jnp.concatenate([band[top + t] for t in range(tiles)], axis=1)
        x_high, x_low = split(x)
        dims = (((1,), (1,)), ((), ()))
        y = lax.dot_general(x_high, high_ref[w], dims, preferred_element_type=jnp.float32)
        y += lax.dot_general(x_low, high_ref[w], dims, preferred_element_type=jnp.float32)
        y += lax.dot_general(x_high, low_ref[w], dims, preferred_element_type=jnp.float32)
        for t in range(tiles):
            band[top + t] = y[:, t * lanes : (t + 1) * lanes]
        return 0

    lax.fori_loop(0, wins, window, 0)
    for part in range(parts):
        for cycle in range(cycles):
            out[part, cycle] = band[cycle * parts + part]


def right(scalars, high, low, picked):
    parts, cycles, rows, lanes = picked.shape
    wins, win, _ = high.shape
    vmem = pl.BlockSpec(memory_space=pltpu.VMEM)
    return pl.pallas_call(
        right_kernel,
        in_specs=[pl.BlockSpec(memory_space=pltpu.SMEM), vmem, vmem, vmem],
        out_specs=vmem,
        out_shape=jax.ShapeDtypeStruct(picked.shape, picked.dtype),
        scratch_shapes=[pltpu.VMEM((parts * cycles, rows, lanes), jnp.float32)],
        compiler_params=pltpu.CompilerParams(vmem_limit_bytes=40 << 20),
        cost_estimate=pl.CostEstimate(
            flops=6 * wins * win * win * rows,
            bytes_accessed=8 * picked.size + 4 * wins * win * win,
            transcendentals=0,
        ),
        name="right",
    )(scalars, high, low, picked)


def body(matrix, factors, starts):
    peers = lax.axis_size("row")
    parts = lax.axis_size("col")
    me = lax.axis_index("row")
    place = lax.axis_index("col")
    cycles, _, tile, width, _, lanes = matrix.shape
    first = starts[0] // tile
    scalars = jnp.stack([me.astype(jnp.int32), first.astype(jnp.int32)])
    each = width // peers
    chunks = CHUNKS if each % (8 * CHUNKS) == 0 else 1
    span = each // chunks
    near = -(-cycles * peers // parts)
    tiles = matrix.reshape(cycles, tile, peers, chunks, span, lanes)

    turned = jnp.swapaxes(factors, 1, 2)
    gathered = lax.all_gather(turned, "col", axis=0)
    high, low = prepare(gathered)

    head = tiles[:, :, 0, 0]
    rows = cycles * tile // parts
    front = head[:, :, :near].reshape(parts, rows, near, lanes)
    front = jnp.swapaxes(front, 1, 2)
    front = lax.all_to_all(front, "col", split_axis=0, concat_axis=0, tiled=True)
    front = right(scalars, high, low, front)
    front = lax.all_to_all(front, "col", split_axis=0, concat_axis=0, tiled=True)
    front = jnp.swapaxes(front, 1, 2).reshape(cycles, tile, near, lanes)
    head = jnp.concatenate([front, head[:, :, near:]], axis=2)

    def piece(owner, chunk):
        value = lax.dynamic_index_in_dim(tiles, owner, 2, keepdims=False)[:, :, chunk]
        if chunk == 0:
            value = jnp.where(owner == 0, head, value)
        return value

    def swap(value, offset):
        return lax.ppermute(value, "row", [(i, i ^ offset) for i in range(peers)])

    order = list(range(1, chunks)) + [0]
    result = tiles
    for chunk in order:
        pieces = [piece(me, chunk)]
        pieces += [swap(piece(jnp.bitwise_xor(me, offset), chunk), offset) for offset in range(1, peers)]
        pieces = left(scalars, high, low, pieces)
        for offset in range(peers):
            value = pieces[offset] if offset == 0 else swap(pieces[offset], offset)
            owner = jnp.bitwise_xor(me, offset)
            result = lax.dynamic_update_slice(
                result, value[:, :, None, None], (0, 0, owner, chunk, 0, 0)
            )
    return result.reshape(matrix.shape)


def solution(mesh):
    placed = (P(None, "row", None, None, "col", None), P(None, None, "col"), P())
    return jax.shard_map(
        body,
        mesh=mesh,
        in_specs=placed,
        out_specs=P(None, "row", None, None, "col", None),
        check_vma=False,
    )
```
